128 devices in a mesh: dp: 2 (over core), ctx: 64 (over z, x, y).
Axes of the slice: x: 4, y: 4, z: 4, core: 2. Of those that a mesh axis runs over, the one named last changes fastest.
Arguments:
- tokens: bfloat16 [32768, 4096], P(('dp', 'ctx')), parts along dimension 0, may hold values from -6 to 19
- positions: int32 [32768], P('dp'), parts along dimension 0, may hold values from 0 to 16383, as said below
- lengths: int32 [256], P('dp'), parts along dimension 0, may hold values from 1 to 384, 16384 in all
- gain: bfloat16 [4096], replicated, may hold values from 0.5 to 1.5
- w_query: bfloat16 [4096, 2048], replicated, may hold values from -0.09375 to 0.09375
- w_key: bfloat16 [4096, 512], replicated, may hold values from -0.09375 to 0.09375
- value_weight: bfloat16 [4096, 512], replicated, may hold values from -0.09375 to 0.09375
Outputs:
- attended: bfloat16 [32768, 2048], P(('dp', 'ctx')), parts along dimension 0
The draws below stay inside these ranges and needn't reach their ends.
There are 2 independent parts, one for each index of `dp`. The reference program is written for one: setup_inputs(seed, part) draws one part's arguments, and reference() takes and returns one part's arrays. A program takes and returns all parts, laid end to end along the dimension named above; an argument that names none is the same for every part. Nothing has to cross between parts.
Inputs may be any that keep to these rules, and one draw needn't show every extreme that they name: positions is a permutation; every aligned block of 256 rows holds exactly 4 positions of each owner j, whose positions are j * 128 to j * 128 + 127 and (2 * 64 - 1 - j) * 128 to (2 * 64 - j) * 128 - 1.
All inputs are finite; a program needn't handle non-finite values.
Results may differ from the reference program's by a relative error of at most 0.012.
The reference program's roundings to bfloat16 on the way count: a program that leaves them out, or rounds other values in their place, can miss the bound.
Values may be sent and summed in bfloat16 or wider, within the bound.
A program may use at most 128 MiB of HBM per device.

```python
import math
import jax
import jax.numpy as jnp
import numpy as np
from jax import lax

MODEL_WIDTH = 4096
HEAD_SIZE = 128
QUERY_HEADS = 16
KEY_VALUE_HEADS = 4
TOK_DEV = 256
TOKENS = 16384
CH = 128
G = 4
NDOCS = 128
DOC_MOST = 384
N_CTX = 64


def zig_table():
    owner = jnp.arange(N_CTX, dtype=jnp.int32)[:, None]
    inner = jnp.arange(TOK_DEV, dtype=jnp.int32)[None, :]
    return jnp.where(inner < CH, owner * CH + inner, (2 * N_CTX - 1 - owner) * CH + inner - CH)


def position_law(key):
    table = zig_table()
    first_key, second_key = jax.random.split(jax.random.fold_in(key, 17))
    first_perm = jax.vmap(lambda sub: jax.random.permutation(sub, TOK_DEV))(jax.random.split(first_key, N_CTX))
    shuffled = jnp.take_along_axis(table, first_perm.astype(jnp.int32), axis=1)
    sources = shuffled.reshape(N_CTX, N_CTX, G).transpose(1, 0, 2).reshape(N_CTX, TOK_DEV)
    second_perm = jax.vmap(lambda sub: jax.random.permutation(sub, TOK_DEV))(jax.random.split(second_key, N_CTX))
    mixed = jnp.take_along_axis(sources, second_perm.astype(jnp.int32), axis=1)
    return mixed.reshape(TOKENS).astype(jnp.int32)


def draw_positions(key, part):
    return position_law(key)


def draw_tokens(key, part):
    unmodified_rows = jax.random.truncated_normal(jax.random.fold_in(key, 23), -6.0, 6.0, (TOKENS, MODEL_WIDTH), jnp.float32)
    return unmodified_rows.astype(jnp.bfloat16)


def draw_w_query(key, part):
    score_scale = MODEL_WIDTH ** (-0.5)
    unmodified_rows = jax.random.truncated_normal(jax.random.fold_in(key, 41), -6.0, 6.0, (MODEL_WIDTH, QUERY_HEADS * HEAD_SIZE), jnp.float32) * score_scale
    return unmodified_rows.astype(jnp.bfloat16)


def draw_w_key(key, part):
    score_scale = MODEL_WIDTH ** (-0.5)
    unmodified_rows = jax.random.truncated_normal(jax.random.fold_in(key, 43), -6.0, 6.0, (MODEL_WIDTH, KEY_VALUE_HEADS * HEAD_SIZE), jnp.float32) * score_scale
    return unmodified_rows.astype(jnp.bfloat16)


def split_up(amount, total, most, skew):
    portions = [(1 << 20) // math.isqrt(rank ** skew) + 1 for rank in range(2, amount + 1)]
    surplus, counts = total - most - (amount - 1), [1] * (amount - 1)
    while surplus > 0:
        candidates = [i for i in range(amount - 1) if counts[i] < most]
        pool, left = sum([portions[i] for i in candidates]), surplus
        for i in candidates:
            addition = min(most - counts[i], max(1, left * portions[i] // pool), surplus)
            counts[i] = counts[i] + addition
            surplus = surplus - addition
    return np.array([most] + counts)


def ragged(own_key, count, total, most, slope):
    if count == 2:
        one = jax.random.randint(own_key, (), max(1, total - most), min(most, total - 1) + 1)
        return jnp.stack([one, total - one])
    sizes = jnp.asarray(split_up(count, total, most, slope), jnp.int32)
    pairs = (count - 1) // 2
    giver, receiver = sizes[1:1 + 2 * pairs:2], sizes[2:2 + 2 * pairs:2]
    slack = jnp.minimum(giver - 1, most - receiver)
    shifted = jax.random.randint(jax.random.fold_in(own_key, 1), (pairs,), 0, 1 << 20) % (slack + 1)
    sizes = sizes.at[1:1 + 2 * pairs:2].set(giver - shifted).at[2:2 + 2 * pairs:2].set(receiver + shifted)
    return sizes[jax.random.permutation(jax.random.fold_in(own_key, 2), count)]


def bell_draw(key, shape, scale, most, kind=jnp.bfloat16):
    return jnp.clip(scale * jax.random.normal(key, shape, jnp.float32), -most, most).astype(kind)


def setup_inputs(seed: int = 0, part: int = 0) -> dict:
    seeds = jax.random.split(jax.random.key(seed), 8)
    own_keys = jax.random.split(jax.random.fold_in(seeds[7], part), 8)
    tokens = draw_tokens(jax.random.fold_in(jax.random.fold_in(seeds[7], part), 71), part)
    positions = draw_positions(jax.random.fold_in(jax.random.fold_in(seeds[7], part), 71), part)
    lengths = ragged(own_keys[2], NDOCS, TOKENS, DOC_MOST, 2).astype(jnp.int32)
    gain = jnp.clip(1.0 + 0.1 * jax.random.normal(seeds[3], (MODEL_WIDTH,), jnp.float32), 0.5, 1.5).astype(jnp.bfloat16)
    w_query = draw_w_query(jax.random.fold_in(seeds[7], 71), part)
    w_key = draw_w_key(jax.random.fold_in(seeds[7], 71), part)
    value_weight = bell_draw(seeds[6], (MODEL_WIDTH, KEY_VALUE_HEADS * HEAD_SIZE), MODEL_WIDTH ** -0.5, 0.09375)
    return dict(tokens=tokens, positions=positions, lengths=lengths, gain=gain, w_query=w_query, w_key=w_key, value_weight=value_weight)


ROPE_THETA = 500000.0
EPSILON = 1e-05

def rope(values, where_at):
    heads = values.shape[1] // HEAD_SIZE
    half = HEAD_SIZE // 2
    shaped = values.reshape(values.shape[0], heads, HEAD_SIZE)
    freq = ROPE_THETA ** (-(jnp.arange(half, dtype=jnp.float32) * 2.0 / HEAD_SIZE))
    angle = where_at.astype(jnp.float32)[:, None, None] * freq[None, None, :]
    cosine = jnp.cos(angle)
    sine = jnp.sin(angle)
    first = shaped[..., :half]
    second = shaped[..., half:]
    turned = jnp.concatenate([first * cosine - second * sine, second * cosine + first * sine], axis=-1)
    return turned.reshape(values.shape[0], heads * HEAD_SIZE)

def project(tokens, gain, w_query, w_key, value_weight, where_at):
    floats = tokens.astype(jnp.float32)
    score_scale = lax.rsqrt(lax.optimization_barrier(jnp.mean(floats * floats, axis=-1, keepdims=True)) + EPSILON)
    normed = (floats * score_scale * gain.astype(jnp.float32)).astype(jnp.bfloat16)
    query = rope(jnp.dot(normed, w_query, preferred_element_type=jnp.float32), where_at).astype(jnp.bfloat16)
    key = rope(jnp.dot(normed, w_key, preferred_element_type=jnp.float32), where_at).astype(jnp.bfloat16)
    value = jnp.dot(normed, value_weight, preferred_element_type=jnp.float32).astype(jnp.bfloat16)
    return (query, key, value)

def doc_of(where_at, lengths):
    ends = jnp.cumsum(lengths, dtype=jnp.int32)
    return lax.optimization_barrier(jnp.sum((ends[None, :] <= where_at[:, None]).astype(jnp.int32), axis=1))

def attend(query, key, value, query_at, key_at, key_valid, lengths):
    rows = query.shape[0]
    keys = key.shape[0]
    kv_heads = key.shape[1] // HEAD_SIZE
    group = query.shape[1] // HEAD_SIZE // kv_heads
    query_doc = doc_of(query_at, lengths)
    key_doc = doc_of(key_at, lengths)
    allowed = (key_doc[None, :] == query_doc[:, None]) & (key_at[None, :] <= query_at[:, None]) & key_valid[None, :]
    q_heads = query.astype(jnp.float32).reshape(rows, kv_heads, group, HEAD_SIZE)
    k_heads = key.astype(jnp.float32).reshape(keys, kv_heads, HEAD_SIZE)
    v_heads = value.astype(jnp.float32).reshape(keys, kv_heads, HEAD_SIZE)
    scores = jnp.einsum('rhgd,khd->hgrk', q_heads, k_heads) * (1.0 / HEAD_SIZE ** 0.5)
    scores = jnp.where(allowed[None, None], scores, jnp.float32(-1e+30))
    top = lax.optimization_barrier(jnp.max(scores, axis=-1, keepdims=True))
    weights = jnp.exp(scores - top)
    total = lax.optimization_barrier(jnp.sum(weights, axis=-1))
    rounded = weights.astype(jnp.bfloat16).astype(jnp.float32)
    mixed = jnp.einsum('hgrk,khd->rhgd', rounded, v_heads)
    mixed = mixed / jnp.transpose(total, (2, 0, 1))[..., None]
    return mixed.reshape(rows, kv_heads * group * HEAD_SIZE).astype(jnp.bfloat16)

def reference(tokens, positions, lengths, gain, w_query, w_key, value_weight):
    query, key, value = project(tokens, gain, w_query, w_key, value_weight, positions)
    total_rows = tokens.shape[0]
    loader_row = jnp.zeros((total_rows,), jnp.int32).at[positions].set(jnp.arange(total_rows, dtype=jnp.int32))
    query = query[loader_row]
    key = key[loader_row]
    value = value[loader_row]
    reach = 3 * CH
    block = min(512, total_rows)
    key_pad = jnp.concatenate([jnp.zeros((reach, key.shape[1]), key.dtype), key], axis=0)
    value_pad = jnp.concatenate([jnp.zeros((reach, value.shape[1]), value.dtype), value], axis=0)

    def one_block(index):
        start = (index * block).astype(jnp.int32)
        q_block = lax.dynamic_slice_in_dim(query, start, block, 0)
        k_block = lax.dynamic_slice_in_dim(key_pad, start, reach + block, 0)
        v_block = lax.dynamic_slice_in_dim(value_pad, start, reach + block, 0)
        query_at = start + jnp.arange(block, dtype=jnp.int32)
        key_at = start - reach + jnp.arange(reach + block, dtype=jnp.int32)
        return attend(q_block, k_block, v_block, query_at, key_at, key_at >= 0, lengths)
    blocks = lax.map(one_block, jnp.arange(total_rows // block, dtype=jnp.int32))
    ordered = blocks.reshape(total_rows, QUERY_HEADS * HEAD_SIZE)
    row = jnp.arange(total_rows, dtype=jnp.int32)
    owner = row // TOK_DEV
    inner = row % TOK_DEV
    zig = jnp.where(inner < CH, owner * CH + inner, (2 * N_CTX - 1 - owner) * CH + inner - CH)
    return ordered[zig]
```

```python
import functools

import jax
import jax.numpy as jnp
import numpy as np
from jax import lax
from jax.experimental import pallas as pl
from jax.experimental.pallas import tpu as pltpu
from jax.sharding import PartitionSpec as P

HEAD = 128
BLOCK = 128
ROPE_THETA = 500000.0
EPSILON = 1e-05
MASKED = -1e30
GROUP = 4
REACH = 3 * BLOCK
RUN = GROUP * BLOCK
MESH = pl.DeviceIdType.MESH
F32 = jnp.float32
BF16 = jnp.bfloat16
I32 = jnp.int32


def iota(shape, axis):
    return lax.broadcasted_iota(I32, shape, axis)


def column_of(row):
    n = row.shape[1]
    eye = iota((n, n), 0) == iota((n, n), 1)
    return jnp.sum(jnp.where(eye, row, 0), axis=1, keepdims=True)


def row_of(column):
    n = column.shape[0]
    eye = iota((n, n), 0) == iota((n, n), 1)
    return jnp.sum(jnp.where(eye, column, 0), axis=0, keepdims=True)


def kernel(
    n,
    tokens,
    positions,
    lengths,
    gain,
    freq,
    w_query,
    w_key,
    w_value,
    out,
    x,
    normed,
    xs,
    perm,
    wbuf,
    cosine,
    sine,
    send,
    recv,
    code,
    slot,
    slot_row,
    onehot,
    kv,
    bias,
    qs,
    osend,
    tok_sem,
    w_sem,
    send_sem,
    recv_sem,
    halo_send,
    halo_recv,
    out_send,
    out_recv,
):
    groups = n // GROUP
    rows, width = tokens.shape
    per = rows // groups
    total = n * per
    me = lax.axis_index("ctx")
    mine = lax.div(me, GROUP)
    head = lax.rem(me, GROUP)

    tok_chunks = tok_sem.shape[0]
    tok_rows = rows // tok_chunks

    def tok_copy(c):
        part = pl.ds(c * tok_rows, tok_rows)
        return pltpu.make_async_copy(tokens.at[part], x.at[part], tok_sem.at[c])

    for c in range(tok_chunks):
        tok_copy(c).start()

    def head_at(i):
        return lax.rem(head + i, GROUP)

    for i in range(GROUP):
        at = pl.ds(pl.multiple_of(head_at(i) * HEAD, HEAD), HEAD)
        pltpu.make_async_copy(w_key.at[:, at], wbuf.at[i, :, pl.ds(0, HEAD)], w_sem.at[i]).start()
        pltpu.make_async_copy(w_value.at[:, at], wbuf.at[i, :, pl.ds(HEAD, HEAD)], w_sem.at[i]).start()
    for t in (1, 2):
        for i in range(GROUP):
            at = pl.ds(pl.multiple_of(head_at(i) * 4 * HEAD + (t - 1) * 2 * HEAD, 2 * HEAD), 2 * HEAD)
            k = t * GROUP + i
            pltpu.make_async_copy(w_query.at[:, at], wbuf.at[k], w_sem.at[k]).start()

    barrier = pltpu.get_barrier_semaphore()

    def greet(r, carry):
        pl.semaphore_signal(
            barrier, inc=1, device_id={"ctx": lax.rem(me + r, n)}, device_id_type=MESH
        )
        return carry

    lax.fori_loop(1, n, greet, 0)

    def group_of(where):
        block = lax.shift_right_logical(where, 7)
        return lax.shift_right_logical(jnp.minimum(block, 2 * n - 1 - block), 2)

    here = jnp.concatenate(
        [positions[pl.ds(2 * me, 1), :], positions[pl.ds(2 * me + 1, 1), :]], axis=1
    )
    group_row = group_of(here)
    group_col = column_of(group_row)
    before = (group_col == group_row) & (iota((rows, rows), 0) < iota((rows, rows), 1))
    rank = group_row * per + jnp.sum(before.astype(I32), axis=0, keepdims=True)
    chosen = iota((rows, rows), 0) == rank
    perm[...] = chosen.astype(F32).astype(BF16)
    where_at = jnp.sum(jnp.where(chosen, here, 0), axis=1, keepdims=True)
    angle = where_at.astype(F32) * freq[...]
    sign = jnp.where(iota((1, HEAD), 1) < HEAD // 2, -1.0, 1.0)
    cosine[...] = jnp.cos(angle)
    sine[...] = jnp.sin(angle) * sign

    tiles = width // HEAD
    for c in range(tok_chunks):
        tok_copy(c).wait()
        part = pl.ds(c * tok_rows, tok_rows)
        square = jnp.zeros((tok_rows, HEAD), F32)
        for j in range(tiles):
            v = x[part, pl.ds(j * HEAD, HEAD)].astype(F32)
            square = square + v * v
        mean = jnp.sum(square, axis=1, keepdims=True) * (1.0 / width)
        scale = lax.rsqrt(mean + EPSILON)
        for j in range(tiles):
            at = pl.ds(j * HEAD, HEAD)
            v = x[part, at].astype(F32) * scale * gain[:, at].astype(F32)
            normed[part, at] = v.astype(BF16)
    step = min(512, width)
    for j in range(width // step):
        at = pl.ds(j * step, step)
        xs[:, at] = jnp.dot(perm[...], normed[:, at], preferred_element_type=F32).astype(BF16)

    def message(t, i, r):
        g = lax.rem(mine + r, groups)
        return send.at[t, i, g], g * GROUP + head_at(i)

    pl.semaphore_wait(barrier, n - 1)

    for t in range(3):

        def project(i, carry, t=t):
            k = t * GROUP + i
            pltpu.make_async_copy(wbuf.at[k], wbuf.at[k], w_sem.at[k]).wait()
            got = jnp.dot(xs[...], wbuf[k], preferred_element_type=F32)
            for c in range(2):
                u = got[:, c * HEAD : (c + 1) * HEAD]
                if t > 0 or c == 0:
                    u = u * cosine[...] + pltpu.roll(u, HEAD // 2, axis=1) * sine[...]
                send[t, i, :, c] = u.astype(BF16).reshape(groups, per, HEAD)

            def post(r, carry):
                src, dest = message(t, i, r)
                pltpu.make_async_remote_copy(
                    src_ref=src,
                    dst_ref=recv.at[t, me],
                    send_sem=send_sem.at[t],
                    recv_sem=recv_sem.at[t],
                    device_id={"ctx": dest},
                    device_id_type=MESH,
                ).start()
                return carry

            lax.fori_loop(1, groups, post, 0)

            @pl.when(i > 0)
            def _():
                post(0, 0)

            @pl.when(i == 0)
            def _():
                src, _ = message(t, i, 0)
                pltpu.make_async_copy(src, recv.at[t, me], recv_sem.at[t]).start()

            return carry

        lax.fori_loop(0, GROUP, project, 0)

    low_base = mine * RUN
    high_base = (2 * n - GROUP - GROUP * mine) * BLOCK
    table = positions[...]
    tall = table.shape[0]
    member = group_of(table) == mine
    ones = member.astype(F32)
    upper = (iota((BLOCK, BLOCK), 0) < iota((BLOCK, BLOCK), 1)).astype(F32).astype(BF16)
    ahead = jnp.dot(ones.astype(BF16), upper, preferred_element_type=F32)
    count = jnp.broadcast_to(jnp.sum(ones, axis=1, keepdims=True), ones.shape)
    odd = lax.rem(iota((tall, BLOCK), 0), 2) == 1
    ahead = ahead + jnp.where(odd, pltpu.roll(count, 1, axis=0), 0.0)
    code[...] = jnp.where(member, ahead.astype(I32), -1)
    slot[...] = jnp.where(table < n * BLOCK, table - low_base, table - high_base + RUN)
    together = BLOCK // per
    kth = iota((per, BLOCK), 0)

    def place(b, carry):
        parts = []
        for q in range(together):
            s = b * together + q
            found = jnp.zeros((per, BLOCK), I32)
            for e in range(2):
                line = pl.ds(2 * s + e, 1)
                found = found + jnp.where(code[line, :] == kth, slot[line, :], 0)
            parts.append(jnp.sum(found, axis=1, keepdims=True))
        column = parts[0] if together == 1 else jnp.concatenate(parts, axis=0)
        slot_row[pl.ds(b, 1), :] = row_of(column)
        return carry

    lax.fori_loop(0, total // BLOCK, place, 0)

    def spread(b, carry):
        first = pl.multiple_of(b * BLOCK, BLOCK)
        want = iota((BLOCK, BLOCK), 0) + first
        for j in range(total // BLOCK):
            hit = want == slot_row[pl.ds(j, 1), :]
            onehot[pl.ds(first, BLOCK), pl.ds(j * BLOCK, BLOCK)] = hit.astype(F32).astype(BF16)
        return carry

    lax.fori_loop(0, total // BLOCK, spread, 0)

    length_col = column_of(lengths[...])
    docs = lengths.shape[1]
    ends = jnp.sum(
        jnp.where(iota((docs, docs), 0) <= iota((docs, docs), 1), length_col, 0), axis=0, keepdims=True
    )
    for run, base in ((0, low_base), (1, high_base)):

        def fill(b, carry, run=run, base=base):
            at = base + b * BLOCK + iota((BLOCK, 1), 0)
            start = jnp.max(jnp.where(ends <= at, ends, 0), axis=1, keepdims=True)
            key = iota((BLOCK, REACH + BLOCK), 1)
            open_ = (key <= REACH + iota((BLOCK, REACH + BLOCK), 0)) & (
                key >= start - (base + b * BLOCK - REACH)
            )
            bias[run, b] = jnp.where(open_, 0.0, MASKED)
            return carry

        lax.fori_loop(0, GROUP, fill, 0)

    def arrived(t):
        pltpu.make_async_copy(recv.at[t], recv.at[t], recv_sem.at[t]).wait()
        both = jnp.concatenate(
            [recv[t, :, c].reshape(total, HEAD) for c in range(2)], axis=1
        )
        return both

    both = arrived(0)
    for run in range(2):
        got = jnp.dot(
            onehot[pl.ds(run * RUN, RUN), :], both, preferred_element_type=F32
        ).astype(BF16)
        for c in range(2):
            kv[run, c, pl.ds(REACH, RUN), :] = got[:, c * HEAD : (c + 1) * HEAD]

    tail = pl.ds(RUN, REACH)
    lead = pl.ds(0, REACH)

    def halo(run, dest):
        return pltpu.make_async_remote_copy(
            src_ref=kv.at[run, :, tail],
            dst_ref=kv.at[run, :, lead],
            send_sem=halo_send.at[run],
            recv_sem=halo_recv.at[run],
            device_id={"ctx": dest},
            device_id_type=MESH,
        )

    last = groups - 1

    @pl.when(mine < last)
    def _():
        halo(0, me + GROUP).start()

    @pl.when(mine > 0)
    def _():
        halo(1, me - GROUP).start()

    @pl.when(mine == last)
    def _():
        pltpu.make_async_copy(kv.at[0, :, tail], kv.at[1, :, lead], halo_recv.at[1]).start()

    @pl.when(mine == 0)
    def _():
        for c in range(2):
            kv[0, c, lead, :] = jnp.zeros((REACH, HEAD), BF16)

    factor = np.float32(np.log2(np.e) / HEAD**0.5)

    def out_copy(t, owner, run):
        src = osend.at[t - 1, owner, run]
        dst = out.at[
            pl.ds(run * BLOCK, BLOCK),
            pl.ds(pl.multiple_of(head * 4 * HEAD + (t - 1) * 2 * HEAD, 2 * HEAD), 2 * HEAD),
        ]
        return src, dst

    for t in (1, 2):
        both = arrived(t)
        for run in range(2):
            got = jnp.dot(
                onehot[pl.ds(run * RUN, RUN), :], both, preferred_element_type=F32
            ).astype(BF16)
            for c in range(2):
                qs[run, c] = got[:, c * HEAD : (c + 1) * HEAD]
        if t == 1:

            @pl.when(mine > 0)
            def _():
                halo(0, me).wait_recv()

            halo(1, me).wait_recv()

        def attend(i, carry, t=t):
            owner = lax.rem(head + 1 + i, GROUP)
            for run in range(2):
                b = owner if run == 0 else GROUP - 1 - owner
                first = pl.multiple_of(b * BLOCK, BLOCK)
                key = kv[run, 0, pl.ds(first, REACH + BLOCK), :]
                value = kv[run, 1, pl.ds(first, REACH + BLOCK), :]
                query = jnp.concatenate([qs[run, c, pl.ds(first, BLOCK), :] for c in range(2)], axis=0)
                s = lax.dot_general(
                    query, key, (((1,), (1,)), ((), ())), preferred_element_type=F32
                )
                mask = bias[run, b]
                s = s + jnp.concatenate([mask, mask], axis=0)
                top = jnp.max(s, axis=1, keepdims=True)
                weights = jnp.exp2((s - top) * factor)
                mass = jnp.sum(weights, axis=1, keepdims=True)
                mixed = jnp.dot(weights.astype(BF16), value, preferred_element_type=F32)
                mixed = (mixed / mass).astype(BF16)
                for c in range(2):
                    osend[t - 1, owner, run, :, pl.ds(c * HEAD, HEAD)] = mixed[
                        c * BLOCK : (c + 1) * BLOCK
                    ]
            for run in range(2):
                src, dst = out_copy(t, owner, run)

                @pl.when(i < GROUP - 1)
                def _(src=src, dst=dst):
                    pltpu.make_async_remote_copy(
                        src_ref=src,
                        dst_ref=dst,
                        send_sem=out_send,
                        recv_sem=out_recv,
                        device_id={"ctx": mine * GROUP + owner},
                        device_id_type=MESH,
                    ).start()

                @pl.when(i == GROUP - 1)
                def _(src=src, dst=dst):
                    pltpu.make_async_copy(src, dst, out_recv).start()

            return carry

        lax.fori_loop(0, GROUP, attend, 0)

    pltpu.make_async_copy(out, out, out_recv).wait()
    sent = osend.at[:, pl.ds(0, GROUP - 1)]
    pltpu.make_async_copy(sent, sent, out_send).wait()

    @pl.when(mine < last)
    def _():
        halo(0, me).wait_send()

    @pl.when(mine > 0)
    def _():
        halo(1, me).wait_send()

    for t in range(3):
        done = recv.at[t, pl.ds(0, n - 1)]
        pltpu.make_async_copy(done, done, send_sem.at[t]).wait()


def shards(n, tokens, positions, lengths, gain, w_query, w_key, value_weight):
    rows, width = tokens.shape
    groups = n // GROUP
    per = rows // groups
    total = n * per
    half = HEAD // 2
    freq = (
        np.float32(ROPE_THETA) ** (-(np.arange(half, dtype=np.float32) * 2.0 / HEAD))
    ).astype(np.float32)
    freq = jnp.asarray(np.concatenate([freq, freq])[None])
    vmem = pl.BlockSpec(memory_space=pltpu.VMEM)
    anywhere = pl.BlockSpec(memory_space=pl.ANY)
    sem = pltpu.SemaphoreType.DMA
    return pl.pallas_call(
        functools.partial(kernel, n),
        name="attention",
        out_shape=jax.ShapeDtypeStruct((rows, w_query.shape[1]), BF16),
        in_specs=[anywhere, vmem, vmem, vmem, vmem, anywhere, anywhere, anywhere],
        out_specs=anywhere,
        scratch_shapes=[
            pltpu.VMEM((rows, width), BF16),
            pltpu.VMEM((rows, width), BF16),
            pltpu.VMEM((rows, width), BF16),
            pltpu.VMEM((rows, rows), BF16),
            pltpu.VMEM((3 * GROUP, width, 2 * HEAD), BF16),
            pltpu.VMEM((rows, HEAD), F32),
            pltpu.VMEM((rows, HEAD), F32),
            pltpu.VMEM((3, GROUP, groups, 2, per, HEAD), BF16),
            pltpu.VMEM((3, n, 2, per, HEAD), BF16),
            pltpu.VMEM((2 * n, BLOCK), I32),
            pltpu.VMEM((2 * n, BLOCK), I32),
            pltpu.VMEM((total // BLOCK, BLOCK), I32),
            pltpu.VMEM((total, total), BF16),
            pltpu.VMEM((2, 2, REACH + RUN, HEAD), BF16),
            pltpu.VMEM((2, GROUP, BLOCK, REACH + BLOCK), F32),
            pltpu.VMEM((2, 2, RUN, HEAD), BF16),
            pltpu.VMEM((2, GROUP, 2, BLOCK, 2 * HEAD), BF16),
            sem((4,)),
            sem((3 * GROUP,)),
            sem((3,)),
            sem((3,)),
            sem((2,)),
            sem((2,)),
            sem,
            sem,
        ],
        compiler_params=pltpu.CompilerParams(
            collective_id=0, has_side_effects=True, vmem_limit_bytes=60 * 1024 * 1024
        ),
    )(
        tokens,
        positions.reshape(2 * n, BLOCK),
        lengths.reshape(1, lengths.shape[0]),
        gain.reshape(1, width),
        freq,
        w_query,
        w_key,
        value_weight,
    )


def solution(mesh):
    in_specs = (P(("dp", "ctx"), None), P("dp"), P("dp"), P(), P(), P(), P())
    out_specs = P(("dp", "ctx"), None)
    return jax.shard_map(
        functools.partial(shards, mesh.shape["ctx"]),
        mesh=mesh,
        in_specs=in_specs,
        out_specs=out_specs,
        check_vma=False,
    )
```

```python
import functools

import jax
import jax.numpy as jnp
import numpy as np
from jax import lax
from jax.experimental import pallas as pl
from jax.experimental.pallas import tpu as pltpu
from jax.sharding import PartitionSpec as P

HEAD = 128
BLOCK = 128
ROPE_THETA = 500000.0
EPSILON = 1e-05
MASKED = -1e30
GROUP = 4
AHEAD = 2
REACH = 3 * BLOCK
RUN = GROUP * BLOCK
MESH = pl.DeviceIdType.MESH
F32 = jnp.float32
BF16 = jnp.bfloat16
I32 = jnp.int32


def iota(shape, axis):
    return lax.broadcasted_iota(I32, shape, axis)


def column_of(row):
    n = row.shape[1]
    eye = iota((n, n), 0) == iota((n, n), 1)
    return jnp.sum(jnp.where(eye, row, 0), axis=1, keepdims=True)


def row_of(column):
    n = column.shape[0]
    eye = iota((n, n), 0) == iota((n, n), 1)
    return jnp.sum(jnp.where(eye, column, 0), axis=0, keepdims=True)


def kernel(
    n,
    tokens,
    positions,
    lengths,
    gain,
    freq,
    w_query,
    w_key,
    w_value,
    out,
    x,
    normed,
    xs,
    perm,
    wbuf,
    cosine,
    sine,
    send,
    recv,
    code,
    slot,
    slot_row,
    onehot,
    kv,
    bias,
    qs,
    osend,
    tok_sem,
    w_sem,
    send_sem,
    recv_sem,
    halo_send,
    halo_recv,
    out_send,
    out_recv,
):
    groups = n // GROUP
    rows, width = tokens.shape
    per = rows // groups
    total = n * per
    me = lax.axis_index("ctx")
    mine = lax.div(me, GROUP)
    head = lax.rem(me, GROUP)

    tok_chunks = tok_sem.shape[0]
    tok_rows = rows // tok_chunks

    def tok_copy(c):
        part = pl.ds(c * tok_rows, tok_rows)
        return pltpu.make_async_copy(tokens.at[part], x.at[part], tok_sem.at[c])

    for c in range(tok_chunks):
        tok_copy(c).start()

    def head_at(i):
        return lax.rem(head + i, GROUP)

    def fetch(k):
        t, i = divmod(k, GROUP)
        if t == 0:
            at = pl.ds(pl.multiple_of(head_at(i) * HEAD, HEAD), HEAD)
            return [
                pltpu.make_async_copy(w.at[:, at], wbuf.at[k, :, pl.ds(c * HEAD, HEAD)], w_sem.at[k])
                for c, w in enumerate((w_key, w_value))
            ]
        at = pl.ds(pl.multiple_of(head_at(i) * 4 * HEAD + (t - 1) * 2 * HEAD, 2 * HEAD), 2 * HEAD)
        return [pltpu.make_async_copy(w_query.at[:, at], wbuf.at[k], w_sem.at[k])]

    def start(k):
        for copy in fetch(k):
            copy.start()

    for k in range(AHEAD):
        start(k)

    barrier = pltpu.get_barrier_semaphore()

    def greet(r, carry):
        pl.semaphore_signal(
            barrier, inc=1, device_id={"ctx": lax.rem(me + r, n)}, device_id_type=MESH
        )
        return carry

    lax.fori_loop(1, n, greet, 0)

    def group_of(where):
        block = lax.shift_right_logical(where, 7)
        return lax.shift_right_logical(jnp.minimum(block, 2 * n - 1 - block), 2)

    here = jnp.concatenate(
        [positions[pl.ds(2 * me, 1), :], positions[pl.ds(2 * me + 1, 1), :]], axis=1
    )
    group_row = group_of(here)
    group_col = column_of(group_row)
    before = (group_col == group_row) & (iota((rows, rows), 0) < iota((rows, rows), 1))
    rank = group_row * per + jnp.sum(before.astype(I32), axis=0, keepdims=True)
    chosen = iota((rows, rows), 0) == rank
    perm[...] = chosen.astype(F32).astype(BF16)
    where_at = jnp.sum(jnp.where(chosen, here, 0), axis=1, keepdims=True)
    angle = where_at.astype(F32) * freq[...]
    sign = jnp.where(iota((1, HEAD), 1) < HEAD // 2, -1.0, 1.0)
    cosine[...] = jnp.cos(angle)
    sine[...] = jnp.sin(angle) * sign

    tiles = width // HEAD
    gains = gain[...].astype(F32)
    for c in range(tok_chunks):
        tok_copy(c).wait()
        part = pl.ds(c * tok_rows, tok_rows)
        square = jnp.zeros((tok_rows, HEAD), F32)
        for j in range(tiles):
            v = x[part, pl.ds(j * HEAD, HEAD)].astype(F32)
            square = square + v * v
        mean = jnp.sum(square, axis=1, keepdims=True) * (1.0 / width)
        scale = lax.rsqrt(mean + EPSILON)
        for j in range(tiles):
            at = pl.ds(j * HEAD, HEAD)
            v = x[part, at].astype(F32) * scale * gains[j : j + 1]
            normed[part, at] = v.astype(BF16)
    step = min(512, width)
    for j in range(width // step):
        at = pl.ds(j * step, step)
        xs[:, at] = jnp.dot(perm[...], normed[:, at], preferred_element_type=F32).astype(BF16)

    def message(t, i, r):
        g = lax.rem(mine + r, groups)
        return send.at[t, i, g], g * GROUP + head_at(i)

    def dispatch(t, i):
        def post(r, carry):
            src, dest = message(t, i, r)
            pltpu.make_async_remote_copy(
                src_ref=src,
                dst_ref=recv.at[t, me],
                send_sem=send_sem.at[t],
                recv_sem=recv_sem.at[t],
                device_id={"ctx": dest},
                device_id_type=MESH,
            ).start()
            return carry

        lax.fori_loop(1, groups, post, 0)
        if i > 0:
            post(0, 0)
        else:
            src, _ = message(t, i, 0)
            pltpu.make_async_copy(src, recv.at[t, me], recv_sem.at[t]).start()

    for t in range(3):
        for i in range(GROUP):
            k = t * GROUP + i
            pltpu.make_async_copy(wbuf.at[k], wbuf.at[k], w_sem.at[k]).wait()
            if k + AHEAD < 3 * GROUP:
                start(k + AHEAD)
            got = jnp.dot(xs[...], wbuf[k], preferred_element_type=F32)
            for c in range(2):
                u = got[:, c * HEAD : (c + 1) * HEAD]
                if t > 0 or c == 0:
                    u = u * cosine[...] + pltpu.roll(u, HEAD // 2, axis=1) * sine[...]
                send[t, i, :, c] = u.astype(BF16).reshape(groups, per, HEAD)
            if k == GROUP - 1:
                pl.semaphore_wait(barrier, n - 1)
                for j in range(k):
                    dispatch(0, j)
            if k >= GROUP - 1:
                dispatch(t, i)

    low_base = mine * RUN
    high_base = (2 * n - GROUP - GROUP * mine) * BLOCK
    table = positions[...]
    tall = table.shape[0]
    member = group_of(table) == mine
    ones = member.astype(F32)
    upper = (iota((BLOCK, BLOCK), 0) < iota((BLOCK, BLOCK), 1)).astype(F32).astype(BF16)
    ahead = jnp.dot(ones.astype(BF16), upper, preferred_element_type=F32)
    count = jnp.broadcast_to(jnp.sum(ones, axis=1, keepdims=True), ones.shape)
    odd = lax.rem(iota((tall, BLOCK), 0), 2) == 1
    ahead = ahead + jnp.where(odd, pltpu.roll(count, 1, axis=0), 0.0)
    code[...] = jnp.where(member, ahead.astype(I32), -1)
    slot[...] = jnp.where(table < n * BLOCK, table - low_base, table - high_base + RUN)
    together = BLOCK // per
    kth = iota((per, BLOCK), 0)

    def place(b, carry):
        parts = []
        for q in range(together):
            s = b * together + q
            found = jnp.zeros((per, BLOCK), I32)
            for e in range(2):
                line = pl.ds(2 * s + e, 1)
                found = found + jnp.where(code[line, :] == kth, slot[line, :], 0)
            parts.append(jnp.sum(found, axis=1, keepdims=True))
        column = parts[0] if together == 1 else jnp.concatenate(parts, axis=0)
        slot_row[pl.ds(b, 1), :] = row_of(column)
        return carry

    lax.fori_loop(0, total // BLOCK, place, 0)

    def spread(b, carry):
        first = pl.multiple_of(b * BLOCK, BLOCK)
        want = iota((BLOCK, BLOCK), 0) + first
        for j in range(total // BLOCK):
            hit = want == slot_row[pl.ds(j, 1), :]
            onehot[pl.ds(first, BLOCK), pl.ds(j * BLOCK, BLOCK)] = hit.astype(F32).astype(BF16)
        return carry

    lax.fori_loop(0, total // BLOCK, spread, 0)

    length_col = column_of(lengths[...])
    docs = lengths.shape[1]
    ends = jnp.sum(
        jnp.where(iota((docs, docs), 0) <= iota((docs, docs), 1), length_col, 0), axis=0, keepdims=True
    )
    for run, base in ((0, low_base), (1, high_base)):

        def fill(b, carry, run=run, base=base):
            at = base + b * BLOCK + iota((BLOCK, 1), 0)
            start = jnp.max(jnp.where(ends <= at, ends, 0), axis=1, keepdims=True)
            key = iota((BLOCK, REACH + BLOCK), 1)
            open_ = (key <= REACH + iota((BLOCK, REACH + BLOCK), 0)) & (
                key >= start - (base + b * BLOCK - REACH)
            )
            bias[run, b] = jnp.where(open_, 0.0, MASKED)
            return carry

        lax.fori_loop(0, GROUP, fill, 0)

    def arrived(t):
        pltpu.make_async_copy(recv.at[t], recv.at[t], recv_sem.at[t]).wait()
        both = jnp.concatenate(
            [recv[t, :, c].reshape(total, HEAD) for c in range(2)], axis=1
        )
        return both

    both = arrived(0)
    for run in range(2):
        got = jnp.dot(
            onehot[pl.ds(run * RUN, RUN), :], both, preferred_element_type=F32
        ).astype(BF16)
        for c in range(2):
            kv[run, c, pl.ds(REACH, RUN), :] = got[:, c * HEAD : (c + 1) * HEAD]

    tail = pl.ds(RUN, REACH)
    lead = pl.ds(0, REACH)

    def halo(run, dest):
        return pltpu.make_async_remote_copy(
            src_ref=kv.at[run, :, tail],
            dst_ref=kv.at[run, :, lead],
            send_sem=halo_send.at[run],
            recv_sem=halo_recv.at[run],
            device_id={"ctx": dest},
            device_id_type=MESH,
        )

    last = groups - 1

    @pl.when(mine < last)
    def _():
        halo(0, me + GROUP).start()

    @pl.when(mine > 0)
    def _():
        halo(1, me - GROUP).start()

    @pl.when(mine == last)
    def _():
        pltpu.make_async_copy(kv.at[0, :, tail], kv.at[1, :, lead], halo_recv.at[1]).start()

    @pl.when(mine == 0)
    def _():
        for c in range(2):
            kv[0, c, lead, :] = jnp.zeros((REACH, HEAD), BF16)

    factor = np.float32(np.log2(np.e) / HEAD**0.5)

    def out_copy(t, owner, run):
        src = osend.at[t - 1, owner, run]
        dst = out.at[
            pl.ds(run * BLOCK, BLOCK),
            pl.ds(pl.multiple_of(head * 4 * HEAD + (t - 1) * 2 * HEAD, 2 * HEAD), 2 * HEAD),
        ]
        return src, dst

    for t in (1, 2):
        both = arrived(t)
        for run in range(2):
            got = jnp.dot(
                onehot[pl.ds(run * RUN, RUN), :], both, preferred_element_type=F32
            ).astype(BF16)
            for c in range(2):
                qs[run, c] = got[:, c * HEAD : (c + 1) * HEAD]
        if t == 1:

            @pl.when(mine > 0)
            def _():
                halo(0, me).wait_recv()

            halo(1, me).wait_recv()

        def attend(i, carry, t=t):
            owner = lax.rem(head + 1 + i, GROUP)
            for run in range(2):
                b = owner if run == 0 else GROUP - 1 - owner
                first = pl.multiple_of(b * BLOCK, BLOCK)
                key = kv[run, 0, pl.ds(first, REACH + BLOCK), :]
                value = kv[run, 1, pl.ds(first, REACH + BLOCK), :]
                query = jnp.concatenate([qs[run, c, pl.ds(first, BLOCK), :] for c in range(2)], axis=0)
                s = lax.dot_general(
                    query, key, (((1,), (1,)), ((), ())), preferred_element_type=F32
                )
                mask = bias[run, b]
                s = s + jnp.concatenate([mask, mask], axis=0)
                top = jnp.max(s, axis=1, keepdims=True)
                weights = jnp.exp2((s - top) * factor)
                mass = jnp.sum(weights, axis=1, keepdims=True)
                mixed = jnp.dot(weights.astype(BF16), value, preferred_element_type=F32)
                mixed = (mixed / mass).astype(BF16)
                for c in range(2):
                    osend[t - 1, owner, run, :, pl.ds(c * HEAD, HEAD)] = mixed[
                        c * BLOCK : (c + 1) * BLOCK
                    ]
            for run in range(2):
                src, dst = out_copy(t, owner, run)

                @pl.when(i < GROUP - 1)
                def _(src=src, dst=dst):
                    pltpu.make_async_remote_copy(
                        src_ref=src,
                        dst_ref=dst,
                        send_sem=out_send,
                        recv_sem=out_recv,
                        device_id={"ctx": mine * GROUP + owner},
                        device_id_type=MESH,
                    ).start()

                @pl.when(i == GROUP - 1)
                def _(src=src, dst=dst):
                    pltpu.make_async_copy(src, dst, out_recv).start()

            return carry

        lax.fori_loop(0, GROUP, attend, 0)

    pltpu.make_async_copy(out, out, out_recv).wait()
    sent = osend.at[:, pl.ds(0, GROUP - 1)]
    pltpu.make_async_copy(sent, sent, out_send).wait()

    @pl.when(mine < last)
    def _():
        halo(0, me).wait_send()

    @pl.when(mine > 0)
    def _():
        halo(1, me).wait_send()

    for t in range(3):
        done = recv.at[t, pl.ds(0, n - 1)]
        pltpu.make_async_copy(done, done, send_sem.at[t]).wait()


def shards(n, tokens, positions, lengths, gain, w_query, w_key, value_weight):
    rows, width = tokens.shape
    groups = n // GROUP
    per = rows // groups
    total = n * per
    half = HEAD // 2
    freq = (
        np.float32(ROPE_THETA) ** (-(np.arange(half, dtype=np.float32) * 2.0 / HEAD))
    ).astype(np.float32)
    freq = jnp.asarray(np.concatenate([freq, freq])[None])
    vmem = pl.BlockSpec(memory_space=pltpu.VMEM)
    anywhere = pl.BlockSpec(memory_space=pl.ANY)
    sem = pltpu.SemaphoreType.DMA
    return pl.pallas_call(
        functools.partial(kernel, n),
        name="attention",
        out_shape=pltpu.VMEM((rows, w_query.shape[1]), BF16),
        in_specs=[anywhere, vmem, vmem, vmem, vmem, anywhere, anywhere, anywhere],
        out_specs=vmem,
        scratch_shapes=[
            pltpu.VMEM((rows, width), BF16),
            pltpu.VMEM((rows, width), BF16),
            pltpu.VMEM((rows, width), BF16),
            pltpu.VMEM((rows, rows), BF16),
            pltpu.VMEM((3 * GROUP, width, 2 * HEAD), BF16),
            pltpu.VMEM((rows, HEAD), F32),
            pltpu.VMEM((rows, HEAD), F32),
            pltpu.VMEM((3, GROUP, groups, 2, per, HEAD), BF16),
            pltpu.VMEM((3, n, 2, per, HEAD), BF16),
            pltpu.VMEM((2 * n, BLOCK), I32),
            pltpu.VMEM((2 * n, BLOCK), I32),
            pltpu.VMEM((total // BLOCK, BLOCK), I32),
            pltpu.VMEM((total, total), BF16),
            pltpu.VMEM((2, 2, REACH + RUN, HEAD), BF16),
            pltpu.VMEM((2, GROUP, BLOCK, REACH + BLOCK), F32),
            pltpu.VMEM((2, 2, RUN, HEAD), BF16),
            pltpu.VMEM((2, GROUP, 2, BLOCK, 2 * HEAD), BF16),
            sem((4,)),
            sem((3 * GROUP,)),
            sem((3,)),
            sem((3,)),
            sem((2,)),
            sem((2,)),
            sem,
            sem,
        ],
        compiler_params=pltpu.CompilerParams(
            collective_id=0, has_side_effects=True, vmem_limit_bytes=60 * 1024 * 1024
        ),
    )(
        tokens,
        positions.reshape(2 * n, BLOCK),
        lengths.reshape(1, lengths.shape[0]),
        gain.reshape(width // HEAD, HEAD),
        freq,
        w_query,
        w_key,
        value_weight,
    )


def solution(mesh):
    in_specs = (P(("dp", "ctx"), None), P("dp"), P("dp"), P(), P(), P(), P())
    out_specs = P(("dp", "ctx"), None)
    return jax.shard_map(
        functools.partial(shards, mesh.shape["ctx"]),
        mesh=mesh,
        in_specs=in_specs,
        out_specs=out_specs,
        check_vma=False,
    )
```

```python
import functools

import jax
import jax.numpy as jnp
import numpy as np
from jax import lax
from jax.experimental import pallas as pl
from jax.experimental.pallas import tpu as pltpu
from jax.sharding import PartitionSpec as P

HEAD = 128
BLOCK = 128
ROPE_THETA = 500000.0
EPSILON = 1e-05
MASKED = -1e30
GROUP = 4
AHEAD = 2
HELD = 2
REACH = 3 * BLOCK
RUN = GROUP * BLOCK
MESH = pl.DeviceIdType.MESH
F32 = jnp.float32
BF16 = jnp.bfloat16
I32 = jnp.int32


def iota(shape, axis):
    return lax.broadcasted_iota(I32, shape, axis)


def column_of(row):
    n = row.shape[1]
    eye = iota((n, n), 0) == iota((n, n), 1)
    return jnp.sum(jnp.where(eye, row, 0), axis=1, keepdims=True)


def row_of(column):
    n = column.shape[0]
    eye = iota((n, n), 0) == iota((n, n), 1)
    return jnp.sum(jnp.where(eye, column, 0), axis=0, keepdims=True)


def kernel(
    n,
    tokens,
    positions,
    lengths,
    gain,
    freq,
    w_query,
    w_key,
    w_value,
    out,
    x,
    normed,
    xs,
    perm,
    wbuf,
    cosine,
    sine,
    send,
    recv,
    code,
    slot,
    slot_row,
    onehot,
    kv,
    bias,
    qs,
    osend,
    tok_sem,
    w_sem,
    send_sem,
    recv_sem,
    halo_send,
    halo_recv,
    out_send,
    out_recv,
):
    groups = n // GROUP
    rows, width = tokens.shape
    per = rows // groups
    total = n * per
    me = lax.axis_index("ctx")
    mine = lax.div(me, GROUP)
    head = lax.rem(me, GROUP)

    tok_chunks = tok_sem.shape[0]
    tok_rows = rows // tok_chunks

    def tok_copy(c):
        part = pl.ds(c * tok_rows, tok_rows)
        return pltpu.make_async_copy(tokens.at[part], x.at[part], tok_sem.at[c])

    for c in range(tok_chunks):
        tok_copy(c).start()

    def head_at(i):
        return lax.rem(head + i, GROUP)

    def fetch(k):
        t, i = divmod(k, GROUP)
        if t == 0:
            at = pl.ds(pl.multiple_of(head_at(i) * HEAD, HEAD), HEAD)
            return [
                pltpu.make_async_copy(w.at[:, at], wbuf.at[k, :, pl.ds(c * HEAD, HEAD)], w_sem.at[k])
                for c, w in enumerate((w_key, w_value))
            ]
        at = pl.ds(pl.multiple_of(head_at(i) * 4 * HEAD + (t - 1) * 2 * HEAD, 2 * HEAD), 2 * HEAD)
        return [pltpu.make_async_copy(w_query.at[:, at], wbuf.at[k], w_sem.at[k])]

    def start(k):
        for copy in fetch(k):
            copy.start()

    for k in range(AHEAD):
        start(k)

    barrier = pltpu.get_barrier_semaphore()

    def greet(r, carry):
        pl.semaphore_signal(
            barrier, inc=1, device_id={"ctx": lax.rem(me + r, n)}, device_id_type=MESH
        )
        return carry

    lax.fori_loop(1, n, greet, 0)

    def group_of(where):
        block = lax.shift_right_logical(where, 7)
        return lax.shift_right_logical(jnp.minimum(block, 2 * n - 1 - block), 2)

    here = jnp.concatenate(
        [positions[pl.ds(2 * me, 1), :], positions[pl.ds(2 * me + 1, 1), :]], axis=1
    )
    group_row = group_of(here)
    group_col = column_of(group_row)
    before = (group_col == group_row) & (iota((rows, rows), 0) < iota((rows, rows), 1))
    rank = group_row * per + jnp.sum(before.astype(I32), axis=0, keepdims=True)
    chosen = iota((rows, rows), 0) == rank
    perm[...] = chosen.astype(F32).astype(BF16)
    where_at = jnp.sum(jnp.where(chosen, here, 0), axis=1, keepdims=True)
    angle = where_at.astype(F32) * freq[...]
    sign = jnp.where(iota((1, HEAD), 1) < HEAD // 2, -1.0, 1.0)
    cosine[...] = jnp.cos(angle)
    sine[...] = jnp.sin(angle) * sign

    tiles = width // HEAD
    gains = gain[...].astype(F32)
    for c in range(tok_chunks):
        tok_copy(c).wait()
        part = pl.ds(c * tok_rows, tok_rows)
        square = jnp.zeros((tok_rows, HEAD), F32)
        for j in range(tiles):
            v = x[part, pl.ds(j * HEAD, HEAD)].astype(F32)
            square = square + v * v
        mean = jnp.sum(square, axis=1, keepdims=True) * (1.0 / width)
        scale = lax.rsqrt(mean + EPSILON)
        for j in range(tiles):
            at = pl.ds(j * HEAD, HEAD)
            v = x[part, at].astype(F32) * scale * gains[j : j + 1]
            normed[part, at] = v.astype(BF16)
    step = min(512, width)
    for j in range(width // step):
        at = pl.ds(j * step, step)
        xs[:, at] = jnp.dot(perm[...], normed[:, at], preferred_element_type=F32).astype(BF16)

    def message(t, i, r):
        g = lax.rem(mine + r, groups)
        return send.at[t, i, g], g * GROUP + head_at(i)

    def dispatch(t, i):
        def post(r, carry):
            src, dest = message(t, i, r)
            pltpu.make_async_remote_copy(
                src_ref=src,
                dst_ref=recv.at[t, me],
                send_sem=send_sem.at[t],
                recv_sem=recv_sem.at[t],
                device_id={"ctx": dest},
                device_id_type=MESH,
            ).start()
            return carry

        lax.fori_loop(1, groups, post, 0)
        if i > 0:
            post(0, 0)
        else:
            src, _ = message(t, i, 0)
            pltpu.make_async_copy(src, recv.at[t, me], recv_sem.at[t]).start()

    low_base = mine * RUN
    high_base = (2 * n - GROUP - GROUP * mine) * BLOCK

    def arrange():
        table = positions[...]
        tall = table.shape[0]
        member = group_of(table) == mine
        ones = member.astype(F32)
        upper = (iota((BLOCK, BLOCK), 0) < iota((BLOCK, BLOCK), 1)).astype(F32).astype(BF16)
        ahead = jnp.dot(ones.astype(BF16), upper, preferred_element_type=F32)
        count = jnp.broadcast_to(jnp.sum(ones, axis=1, keepdims=True), ones.shape)
        odd = lax.rem(iota((tall, BLOCK), 0), 2) == 1
        ahead = ahead + jnp.where(odd, pltpu.roll(count, 1, axis=0), 0.0)
        code[...] = jnp.where(member, ahead.astype(I32), -1)
        slot[...] = jnp.where(table < n * BLOCK, table - low_base, table - high_base + RUN)
        together = BLOCK // per
        kth = iota((per, BLOCK), 0)
        for b in range(total // BLOCK):
            parts = []
            for q in range(together):
                found = jnp.zeros((per, BLOCK), I32)
                for e in range(2):
                    line = pl.ds(2 * (b * together + q) + e, 1)
                    found = found + jnp.where(code[line, :] == kth, slot[line, :], 0)
                parts.append(jnp.sum(found, axis=1, keepdims=True))
            column = parts[0] if together == 1 else jnp.concatenate(parts, axis=0)
            slot_row[pl.ds(b, 1), :] = row_of(column)
        lines = iota((BLOCK, BLOCK), 0).astype(F32).astype(BF16)

        def spread(b, carry):
            first = pl.multiple_of(b * BLOCK, BLOCK)
            for j in range(total // BLOCK):
                want = slot_row[pl.ds(j, 1), :] - first
                want = jnp.where((want >= 0) & (want < BLOCK), want, -1)
                want = jnp.broadcast_to(want, (16, BLOCK)).astype(F32).astype(BF16)
                hit = lines == jnp.concatenate([want] * (BLOCK // 16), axis=0)
                onehot[pl.ds(first, BLOCK), pl.ds(j * BLOCK, BLOCK)] = jnp.where(
                    hit, jnp.ones((), BF16), jnp.zeros((), BF16)
                )
            return carry

        lax.fori_loop(0, total // BLOCK, spread, 0)

    for t in range(3):
        for i in range(GROUP):
            k = t * GROUP + i
            pltpu.make_async_copy(wbuf.at[k], wbuf.at[k], w_sem.at[k]).wait()
            if k + AHEAD < 3 * GROUP:
                start(k + AHEAD)
            got = jnp.dot(xs[...], wbuf[k], preferred_element_type=F32)
            for c in range(2):
                u = got[:, c * HEAD : (c + 1) * HEAD]
                if t > 0 or c == 0:
                    u = u * cosine[...] + pltpu.roll(u, HEAD // 2, axis=1) * sine[...]
                send[t, i, :, c] = u.astype(BF16).reshape(groups, per, HEAD)
            if k == GROUP - 1:
                pl.semaphore_wait(barrier, n - 1)
                for j in range(k):
                    dispatch(0, j)
            if k >= GROUP - 1 and k < 3 * GROUP - HELD:
                dispatch(t, i)
            if k == GROUP - 1:
                arrange()

    def arrived(t):
        pltpu.make_async_copy(recv.at[t], recv.at[t], recv_sem.at[t]).wait()
        both = jnp.concatenate(
            [recv[t, :, c].reshape(total, HEAD) for c in range(2)], axis=1
        )
        return both

    both = arrived(0)
    for run in range(2):
        got = jnp.dot(
            onehot[pl.ds(run * RUN, RUN), :], both, preferred_element_type=F32
        ).astype(BF16)
        for c in range(2):
            kv[run, c, pl.ds(REACH, RUN), :] = got[:, c * HEAD : (c + 1) * HEAD]

    tail = pl.ds(RUN, REACH)
    lead = pl.ds(0, REACH)

    def halo(run, dest):
        return pltpu.make_async_remote_copy(
            src_ref=kv.at[run, :, tail],
            dst_ref=kv.at[run, :, lead],
            send_sem=halo_send.at[run],
            recv_sem=halo_recv.at[run],
            device_id={"ctx": dest},
            device_id_type=MESH,
        )

    last = groups - 1

    @pl.when(mine < last)
    def _():
        halo(0, me + GROUP).start()

    @pl.when(mine > 0)
    def _():
        halo(1, me - GROUP).start()

    @pl.when(mine == last)
    def _():
        pltpu.make_async_copy(kv.at[0, :, tail], kv.at[1, :, lead], halo_recv.at[1]).start()

    @pl.when(mine == 0)
    def _():
        for c in range(2):
            kv[0, c, lead, :] = jnp.zeros((REACH, HEAD), BF16)

    for i in range(GROUP - HELD, GROUP):
        dispatch(2, i)

    length_col = column_of(lengths[...])
    docs = lengths.shape[1]
    ends = jnp.sum(
        jnp.where(iota((docs, docs), 0) <= iota((docs, docs), 1), length_col, 0), axis=0, keepdims=True
    )
    for run, base in ((0, low_base), (1, high_base)):

        def fill(b, carry, run=run, base=base):
            at = base + b * BLOCK + iota((BLOCK, 1), 0)
            start = jnp.max(jnp.where(ends <= at, ends, 0), axis=1, keepdims=True)
            key = iota((BLOCK, REACH + BLOCK), 1)
            open_ = (key <= REACH + iota((BLOCK, REACH + BLOCK), 0)) & (
                key >= start - (base + b * BLOCK - REACH)
            )
            bias[run, b] = jnp.where(open_, 0.0, MASKED)
            return carry

        lax.fori_loop(0, GROUP, fill, 0)

    factor = np.float32(np.log2(np.e) / HEAD**0.5)

    def out_copy(t, owner, run):
        src = osend.at[t - 1, owner, run]
        dst = out.at[
            pl.ds(run * BLOCK, BLOCK),
            pl.ds(pl.multiple_of(head * 4 * HEAD + (t - 1) * 2 * HEAD, 2 * HEAD), 2 * HEAD),
        ]
        return src, dst

    for t in (1, 2):
        both = arrived(t)
        for run in range(2):
            got = jnp.dot(
                onehot[pl.ds(run * RUN, RUN), :], both, preferred_element_type=F32
            ).astype(BF16)
            for c in range(2):
                qs[run, c] = got[:, c * HEAD : (c + 1) * HEAD]
        if t == 1:

            @pl.when(mine > 0)
            def _():
                halo(0, me).wait_recv()

            halo(1, me).wait_recv()

        def attend(i, carry, t=t):
            owner = lax.rem(head + 1 + i, GROUP)
            for run in range(2):
                b = owner if run == 0 else GROUP - 1 - owner
                first = pl.multiple_of(b * BLOCK, BLOCK)
                key = kv[run, 0, pl.ds(first, REACH + BLOCK), :]
                value = kv[run, 1, pl.ds(first, REACH + BLOCK), :]
                query = jnp.concatenate([qs[run, c, pl.ds(first, BLOCK), :] for c in range(2)], axis=0)
                s = lax.dot_general(
                    query, key, (((1,), (1,)), ((), ())), preferred_element_type=F32
                )
                mask = bias[run, b]
                s = s + jnp.concatenate([mask, mask], axis=0)
                top = jnp.max(s, axis=1, keepdims=True)
                weights = jnp.exp2((s - top) * factor)
                mass = jnp.sum(weights, axis=1, keepdims=True)
                mixed = jnp.dot(weights.astype(BF16), value, preferred_element_type=F32)
                mixed = (mixed / mass).astype(BF16)
                for c in range(2):
                    osend[t - 1, owner, run, :, pl.ds(c * HEAD, HEAD)] = mixed[
                        c * BLOCK : (c + 1) * BLOCK
                    ]
            for run in range(2):
                src, dst = out_copy(t, owner, run)

                @pl.when(i < GROUP - 1)
                def _(src=src, dst=dst):
                    pltpu.make_async_remote_copy(
                        src_ref=src,
                        dst_ref=dst,
                        send_sem=out_send,
                        recv_sem=out_recv,
                        device_id={"ctx": mine * GROUP + owner},
                        device_id_type=MESH,
                    ).start()

                @pl.when(i == GROUP - 1)
                def _(src=src, dst=dst):
                    pltpu.make_async_copy(src, dst, out_recv).start()

            return carry

        lax.fori_loop(0, GROUP, attend, 0)

    pltpu.make_async_copy(out, out, out_recv).wait()
    sent = osend.at[:, pl.ds(0, GROUP - 1)]
    pltpu.make_async_copy(sent, sent, out_send).wait()

    @pl.when(mine < last)
    def _():
        halo(0, me).wait_send()

    @pl.when(mine > 0)
    def _():
        halo(1, me).wait_send()

    for t in range(3):
        done = recv.at[t, pl.ds(0, n - 1)]
        pltpu.make_async_copy(done, done, send_sem.at[t]).wait()


def shards(n, tokens, positions, lengths, gain, w_query, w_key, value_weight):
    rows, width = tokens.shape
    groups = n // GROUP
    per = rows // groups
    total = n * per
    half = HEAD // 2
    freq = (
        np.float32(ROPE_THETA) ** (-(np.arange(half, dtype=np.float32) * 2.0 / HEAD))
    ).astype(np.float32)
    freq = jnp.asarray(np.concatenate([freq, freq])[None])
    vmem = pl.BlockSpec(memory_space=pltpu.VMEM)
    anywhere = pl.BlockSpec(memory_space=pl.ANY)
    sem = pltpu.SemaphoreType.DMA
    return pl.pallas_call(
        functools.partial(kernel, n),
        name="attention",
        out_shape=pltpu.VMEM((rows, w_query.shape[1]), BF16),
        in_specs=[anywhere, vmem, vmem, vmem, vmem, anywhere, anywhere, anywhere],
        out_specs=vmem,
        scratch_shapes=[
            pltpu.VMEM((rows, width), BF16),
            pltpu.VMEM((rows, width), BF16),
            pltpu.VMEM((rows, width), BF16),
            pltpu.VMEM((rows, rows), BF16),
            pltpu.VMEM((3 * GROUP, width, 2 * HEAD), BF16),
            pltpu.VMEM((rows, HEAD), F32),
            pltpu.VMEM((rows, HEAD), F32),
            pltpu.VMEM((3, GROUP, groups, 2, per, HEAD), BF16),
            pltpu.VMEM((3, n, 2, per, HEAD), BF16),
            pltpu.VMEM((2 * n, BLOCK), I32),
            pltpu.VMEM((2 * n, BLOCK), I32),
            pltpu.VMEM((total // BLOCK, BLOCK), I32),
            pltpu.VMEM((total, total), BF16),
            pltpu.VMEM((2, 2, REACH + RUN, HEAD), BF16),
            pltpu.VMEM((2, GROUP, BLOCK, REACH + BLOCK), F32),
            pltpu.VMEM((2, 2, RUN, HEAD), BF16),
            pltpu.VMEM((2, GROUP, 2, BLOCK, 2 * HEAD), BF16),
            sem((4,)),
            sem((3 * GROUP,)),
            sem((3,)),
            sem((3,)),
            sem((2,)),
            sem((2,)),
            sem,
            sem,
        ],
        compiler_params=pltpu.CompilerParams(
            collective_id=0, has_side_effects=True, vmem_limit_bytes=60 * 1024 * 1024
        ),
    )(
        tokens,
        positions.reshape(2 * n, BLOCK),
        lengths.reshape(1, lengths.shape[0]),
        gain.reshape(width // HEAD, HEAD),
        freq,
        w_query,
        w_key,
        value_weight,
    )


def solution(mesh):
    in_specs = (P(("dp", "ctx"), None), P("dp"), P("dp"), P(), P(), P(), P())
    out_specs = P(("dp", "ctx"), None)
    return jax.shard_map(
        functools.partial(shards, mesh.shape["ctx"]),
        mesh=mesh,
        in_specs=in_specs,
        out_specs=out_specs,
        check_vma=False,
    )
```

```python
import functools

import jax
import jax.numpy as jnp
import numpy as np
from jax import lax
from jax.experimental import pallas as pl
from jax.experimental.pallas import tpu as pltpu
from jax.sharding import PartitionSpec as P

HEAD = 128
BLOCK = 128
ROPE_THETA = 500000.0
EPSILON = 1e-05
MASKED = -1e30
GROUP = 4
AHEAD = 2
HELD = 2
TURNS = (0, 2, 1, 3)
REACH = 3 * BLOCK
RUN = GROUP * BLOCK
MESH = pl.DeviceIdType.MESH
F32 = jnp.float32
BF16 = jnp.bfloat16
I32 = jnp.int32


def iota(shape, axis):
    return lax.broadcasted_iota(I32, shape, axis)


def column_of(row):
    n = row.shape[1]
    eye = iota((n, n), 0) == iota((n, n), 1)
    return jnp.sum(jnp.where(eye, row, 0), axis=1, keepdims=True)


def row_of(column):
    n = column.shape[0]
    eye = iota((n, n), 0) == iota((n, n), 1)
    return jnp.sum(jnp.where(eye, column, 0), axis=0, keepdims=True)


def kernel(
    n,
    tokens,
    positions,
    lengths,
    gain,
    freq,
    w_query,
    w_key,
    w_value,
    out,
    x,
    normed,
    xs,
    perm,
    wbuf,
    cosine,
    sine,
    send,
    recv,
    code,
    slot,
    slot_row,
    onehot,
    kv,
    bias,
    qs,
    osend,
    tok_sem,
    w_sem,
    send_sem,
    recv_sem,
    halo_send,
    halo_recv,
    out_send,
    out_recv,
):
    groups = n // GROUP
    rows, width = tokens.shape
    per = rows // groups
    total = n * per
    me = lax.axis_index("ctx")
    mine = lax.div(me, GROUP)
    head = lax.rem(me, GROUP)

    tok_chunks = tok_sem.shape[0]
    tok_rows = rows // tok_chunks

    def tok_copy(c):
        part = pl.ds(c * tok_rows, tok_rows)
        return pltpu.make_async_copy(tokens.at[part], x.at[part], tok_sem.at[c])

    for c in range(tok_chunks):
        tok_copy(c).start()

    def head_at(i):
        return lax.rem(head + TURNS[i], GROUP)

    def fetch(k):
        t, i = divmod(k, GROUP)
        if t == 0:
            at = pl.ds(pl.multiple_of(head_at(i) * HEAD, HEAD), HEAD)
            return [
                pltpu.make_async_copy(w.at[:, at], wbuf.at[k, :, pl.ds(c * HEAD, HEAD)], w_sem.at[k])
                for c, w in enumerate((w_key, w_value))
            ]
        at = pl.ds(pl.multiple_of(head_at(i) * 4 * HEAD + (t - 1) * 2 * HEAD, 2 * HEAD), 2 * HEAD)
        return [pltpu.make_async_copy(w_query.at[:, at], wbuf.at[k], w_sem.at[k])]

    def start(k):
        for copy in fetch(k):
            copy.start()

    for k in range(AHEAD):
        start(k)

    barrier = pltpu.get_barrier_semaphore()

    def greet(r, carry):
        pl.semaphore_signal(
            barrier, inc=1, device_id={"ctx": lax.rem(me + r, n)}, device_id_type=MESH
        )
        return carry

    lax.fori_loop(1, n, greet, 0)

    def group_of(where):
        block = lax.shift_right_logical(where, 7)
        return lax.shift_right_logical(jnp.minimum(block, 2 * n - 1 - block), 2)

    here = jnp.concatenate(
        [positions[pl.ds(2 * me, 1), :], positions[pl.ds(2 * me + 1, 1), :]], axis=1
    )
    group_row = group_of(here)
    group_col = column_of(group_row)
    before = (group_col == group_row) & (iota((rows, rows), 0) < iota((rows, rows), 1))
    rank = group_row * per + jnp.sum(before.astype(I32), axis=0, keepdims=True)
    chosen = iota((rows, rows), 0) == rank
    perm[...] = chosen.astype(F32).astype(BF16)
    where_at = jnp.sum(jnp.where(chosen, here, 0), axis=1, keepdims=True)
    angle = where_at.astype(F32) * freq[...]
    sign = jnp.where(iota((1, HEAD), 1) < HEAD // 2, -1.0, 1.0)
    cosine[...] = jnp.cos(angle)
    sine[...] = jnp.sin(angle) * sign

    tiles = width // HEAD
    gains = gain[...].astype(F32)
    for c in range(tok_chunks):
        tok_copy(c).wait()
        part = pl.ds(c * tok_rows, tok_rows)
        square = jnp.zeros((tok_rows, HEAD), F32)
        for j in range(tiles):
            v = x[part, pl.ds(j * HEAD, HEAD)].astype(F32)
            square = square + v * v
        mean = jnp.sum(square, axis=1, keepdims=True) * (1.0 / width)
        scale = lax.rsqrt(mean + EPSILON)
        for j in range(tiles):
            at = pl.ds(j * HEAD, HEAD)
            v = x[part, at].astype(F32) * scale * gains[j : j + 1]
            normed[part, at] = v.astype(BF16)
    step = min(512, width)
    for j in range(width // step):
        at = pl.ds(j * step, step)
        xs[:, at] = jnp.dot(perm[...], normed[:, at], preferred_element_type=F32).astype(BF16)

    def message(t, i, r):
        g = lax.rem(mine + r, groups)
        return send.at[t, i, g], g * GROUP + head_at(i)

    def dispatch(t, i):
        def post(r, carry):
            src, dest = message(t, i, r)
            pltpu.make_async_remote_copy(
                src_ref=src,
                dst_ref=recv.at[t, me],
                send_sem=send_sem.at[t],
                recv_sem=recv_sem.at[t],
                device_id={"ctx": dest},
                device_id_type=MESH,
            ).start()
            return carry

        lax.fori_loop(1, groups, post, 0)
        if i > 0:
            post(0, 0)
        else:
            src, _ = message(t, i, 0)
            pltpu.make_async_copy(src, recv.at[t, me], recv_sem.at[t]).start()

    low_base = mine * RUN
    high_base = (2 * n - GROUP - GROUP * mine) * BLOCK

    def arrange():
        table = positions[...]
        tall = table.shape[0]
        member = group_of(table) == mine
        ones = member.astype(F32)
        upper = (iota((BLOCK, BLOCK), 0) < iota((BLOCK, BLOCK), 1)).astype(F32).astype(BF16)
        ahead = jnp.dot(ones.astype(BF16), upper, preferred_element_type=F32)
        count = jnp.broadcast_to(jnp.sum(ones, axis=1, keepdims=True), ones.shape)
        odd = lax.rem(iota((tall, BLOCK), 0), 2) == 1
        ahead = ahead + jnp.where(odd, pltpu.roll(count, 1, axis=0), 0.0)
        code[...] = jnp.where(member, ahead.astype(I32), -1)
        slot[...] = jnp.where(table < n * BLOCK, table - low_base, table - high_base + RUN)
        together = BLOCK // per
        kth = iota((per, BLOCK), 0)
        for b in range(total // BLOCK):
            parts = []
            for q in range(together):
                found = jnp.zeros((per, BLOCK), I32)
                for e in range(2):
                    line = pl.ds(2 * (b * together + q) + e, 1)
                    found = found + jnp.where(code[line, :] == kth, slot[line, :], 0)
                parts.append(jnp.sum(found, axis=1, keepdims=True))
            column = parts[0] if together == 1 else jnp.concatenate(parts, axis=0)
            slot_row[pl.ds(b, 1), :] = row_of(column)
        lines = iota((BLOCK, BLOCK), 0).astype(F32).astype(BF16)

        def spread(b, carry):
            first = pl.multiple_of(b * BLOCK, BLOCK)
            for j in range(total // BLOCK):
                want = slot_row[pl.ds(j, 1), :] - first
                want = jnp.where((want >= 0) & (want < BLOCK), want, -1)
                want = jnp.broadcast_to(want, (16, BLOCK)).astype(F32).astype(BF16)
                hit = lines == jnp.concatenate([want] * (BLOCK // 16), axis=0)
                onehot[pl.ds(first, BLOCK), pl.ds(j * BLOCK, BLOCK)] = jnp.where(
                    hit, jnp.ones((), BF16), jnp.zeros((), BF16)
                )
            return carry

        lax.fori_loop(0, total // BLOCK, spread, 0)

    for t in range(3):
        for i in range(GROUP):
            k = t * GROUP + i
            pltpu.make_async_copy(wbuf.at[k], wbuf.at[k], w_sem.at[k]).wait()
            if k + AHEAD < 3 * GROUP:
                start(k + AHEAD)
            got = jnp.dot(xs[...], wbuf[k], preferred_element_type=F32)
            for c in range(2):
                u = got[:, c * HEAD : (c + 1) * HEAD]
                if t > 0 or c == 0:
                    u = u * cosine[...] + pltpu.roll(u, HEAD // 2, axis=1) * sine[...]
                send[t, i, :, c] = u.astype(BF16).reshape(groups, per, HEAD)
            if k == GROUP - 1:
                pl.semaphore_wait(barrier, n - 1)
                for j in range(k):
                    dispatch(0, j)
            if k >= GROUP - 1 and k < 3 * GROUP - HELD:
                dispatch(t, i)
            if k == GROUP - 1:
                arrange()

    def arrived(t):
        pltpu.make_async_copy(recv.at[t], recv.at[t], recv_sem.at[t]).wait()
        both = jnp.concatenate(
            [recv[t, :, c].reshape(total, HEAD) for c in range(2)], axis=1
        )
        return both

    both = arrived(0)
    for run in range(2):
        got = jnp.dot(
            onehot[pl.ds(run * RUN, RUN), :], both, preferred_element_type=F32
        ).astype(BF16)
        for c in range(2):
            kv[run, c, pl.ds(REACH, RUN), :] = got[:, c * HEAD : (c + 1) * HEAD]

    tail = pl.ds(RUN, REACH)
    lead = pl.ds(0, REACH)

    def halo(run, dest):
        return pltpu.make_async_remote_copy(
            src_ref=kv.at[run, :, tail],
            dst_ref=kv.at[run, :, lead],
            send_sem=halo_send.at[run],
            recv_sem=halo_recv.at[run],
            device_id={"ctx": dest},
            device_id_type=MESH,
        )

    last = groups - 1

    @pl.when(mine < last)
    def _():
        halo(0, me + GROUP).start()

    @pl.when(mine > 0)
    def _():
        halo(1, me - GROUP).start()

    @pl.when(mine == last)
    def _():
        pltpu.make_async_copy(kv.at[0, :, tail], kv.at[1, :, lead], halo_recv.at[1]).start()

    @pl.when(mine == 0)
    def _():
        for c in range(2):
            kv[0, c, lead, :] = jnp.zeros((REACH, HEAD), BF16)

    for i in range(GROUP - HELD, GROUP):
        dispatch(2, i)

    length_col = column_of(lengths[...])
    docs = lengths.shape[1]
    ends = jnp.sum(
        jnp.where(iota((docs, docs), 0) <= iota((docs, docs), 1), length_col, 0), axis=0, keepdims=True
    )
    for run, base in ((0, low_base), (1, high_base)):

        def fill(b, carry, run=run, base=base):
            at = base + b * BLOCK + iota((BLOCK, 1), 0)
            start = jnp.max(jnp.where(ends <= at, ends, 0), axis=1, keepdims=True)
            key = iota((BLOCK, REACH + BLOCK), 1)
            open_ = (key <= REACH + iota((BLOCK, REACH + BLOCK), 0)) & (
                key >= start - (base + b * BLOCK - REACH)
            )
            bias[run, b] = jnp.where(open_, 0.0, MASKED)
            return carry

        lax.fori_loop(0, GROUP, fill, 0)

    factor = np.float32(np.log2(np.e) / HEAD**0.5)

    def out_copy(t, owner, run):
        src = osend.at[t - 1, owner, run]
        dst = out.at[
            pl.ds(run * BLOCK, BLOCK),
            pl.ds(pl.multiple_of(head * 4 * HEAD + (t - 1) * 2 * HEAD, 2 * HEAD), 2 * HEAD),
        ]
        return src, dst

    for t in (1, 2):
        both = arrived(t)
        for run in range(2):
            got = jnp.dot(
                onehot[pl.ds(run * RUN, RUN), :], both, preferred_element_type=F32
            ).astype(BF16)
            for c in range(2):
                qs[run, c] = got[:, c * HEAD : (c + 1) * HEAD]
        if t == 1:

            @pl.when(mine > 0)
            def _():
                halo(0, me).wait_recv()

            halo(1, me).wait_recv()

        def attend(i, carry, t=t):
            owner = lax.rem(head + 1 + i, GROUP)
            for run in range(2):
                b = owner if run == 0 else GROUP - 1 - owner
                first = pl.multiple_of(b * BLOCK, BLOCK)
                key = kv[run, 0, pl.ds(first, REACH + BLOCK), :]
                value = kv[run, 1, pl.ds(first, REACH + BLOCK), :]
                query = jnp.concatenate([qs[run, c, pl.ds(first, BLOCK), :] for c in range(2)], axis=0)
                s = lax.dot_general(
                    query, key, (((1,), (1,)), ((), ())), preferred_element_type=F32
                )
                mask = bias[run, b]
                s = s + jnp.concatenate([mask, mask], axis=0)
                top = jnp.max(s, axis=1, keepdims=True)
                weights = jnp.exp2((s - top) * factor)
                mass = jnp.sum(weights, axis=1, keepdims=True)
                mixed = jnp.dot(weights.astype(BF16), value, preferred_element_type=F32)
                mixed = (mixed / mass).astype(BF16)
                for c in range(2):
                    osend[t - 1, owner, run, :, pl.ds(c * HEAD, HEAD)] = mixed[
                        c * BLOCK : (c + 1) * BLOCK
                    ]
            for run in range(2):
                src, dst = out_copy(t, owner, run)

                @pl.when(i < GROUP - 1)
                def _(src=src, dst=dst):
                    pltpu.make_async_remote_copy(
                        src_ref=src,
                        dst_ref=dst,
                        send_sem=out_send,
                        recv_sem=out_recv,
                        device_id={"ctx": mine * GROUP + owner},
                        device_id_type=MESH,
                    ).start()

                @pl.when(i == GROUP - 1)
                def _(src=src, dst=dst):
                    pltpu.make_async_copy(src, dst, out_recv).start()

            return carry

        lax.fori_loop(0, GROUP, attend, 0)

    pltpu.make_async_copy(out, out, out_recv).wait()
    sent = osend.at[:, pl.ds(0, GROUP - 1)]
    pltpu.make_async_copy(sent, sent, out_send).wait()

    @pl.when(mine < last)
    def _():
        halo(0, me).wait_send()

    @pl.when(mine > 0)
    def _():
        halo(1, me).wait_send()

    for t in range(3):
        done = recv.at[t, pl.ds(0, n - 1)]
        pltpu.make_async_copy(done, done, send_sem.at[t]).wait()


def shards(n, tokens, positions, lengths, gain, w_query, w_key, value_weight):
    rows, width = tokens.shape
    groups = n // GROUP
    per = rows // groups
    total = n * per
    half = HEAD // 2
    freq = (
        np.float32(ROPE_THETA) ** (-(np.arange(half, dtype=np.float32) * 2.0 / HEAD))
    ).astype(np.float32)
    freq = jnp.asarray(np.concatenate([freq, freq])[None])
    vmem = pl.BlockSpec(memory_space=pltpu.VMEM)
    anywhere = pl.BlockSpec(memory_space=pl.ANY)
    sem = pltpu.SemaphoreType.DMA
    return pl.pallas_call(
        functools.partial(kernel, n),
        name="attention",
        out_shape=pltpu.VMEM((rows, w_query.shape[1]), BF16),
        in_specs=[anywhere, vmem, vmem, vmem, vmem, anywhere, anywhere, anywhere],
        out_specs=vmem,
        scratch_shapes=[
            pltpu.VMEM((rows, width), BF16),
            pltpu.VMEM((rows, width), BF16),
            pltpu.VMEM((rows, width), BF16),
            pltpu.VMEM((rows, rows), BF16),
            pltpu.VMEM((3 * GROUP, width, 2 * HEAD), BF16),
            pltpu.VMEM((rows, HEAD), F32),
            pltpu.VMEM((rows, HEAD), F32),
            pltpu.VMEM((3, GROUP, groups, 2, per, HEAD), BF16),
            pltpu.VMEM((3, n, 2, per, HEAD), BF16),
            pltpu.VMEM((2 * n, BLOCK), I32),
            pltpu.VMEM((2 * n, BLOCK), I32),
            pltpu.VMEM((total // BLOCK, BLOCK), I32),
            pltpu.VMEM((total, total), BF16),
            pltpu.VMEM((2, 2, REACH + RUN, HEAD), BF16),
            pltpu.VMEM((2, GROUP, BLOCK, REACH + BLOCK), F32),
            pltpu.VMEM((2, 2, RUN, HEAD), BF16),
            pltpu.VMEM((2, GROUP, 2, BLOCK, 2 * HEAD), BF16),
            sem((4,)),
            sem((3 * GROUP,)),
            sem((3,)),
            sem((3,)),
            sem((2,)),
            sem((2,)),
            sem,
            sem,
        ],
        compiler_params=pltpu.CompilerParams(
            collective_id=0, has_side_effects=True, vmem_limit_bytes=60 * 1024 * 1024
        ),
    )(
        tokens,
        positions.reshape(2 * n, BLOCK),
        lengths.reshape(1, lengths.shape[0]),
        gain.reshape(width // HEAD, HEAD),
        freq,
        w_query,
        w_key,
        value_weight,
    )


def solution(mesh):
    in_specs = (P(("dp", "ctx"), None), P("dp"), P("dp"), P(), P(), P(), P())
    out_specs = P(("dp", "ctx"), None)
    return jax.shard_map(
        functools.partial(shards, mesh.shape["ctx"]),
        mesh=mesh,
        in_specs=in_specs,
        out_specs=out_specs,
        check_vma=False,
    )
```

```python
import functools

import jax
import jax.numpy as jnp
import numpy as np
from jax import lax
from jax.experimental import pallas as pl
from jax.experimental.pallas import tpu as pltpu
from jax.sharding import PartitionSpec as P

HEAD = 128
BLOCK = 128
ROPE_THETA = 500000.0
EPSILON = 1e-05
MASKED = -1e30
GROUP = 4
AHEAD = 2
HELD = 2
HALO_ROWS = 64
OUT_ROWS = 32
TURNS = (0, 2, 1, 3)
REACH = 3 * BLOCK
RUN = GROUP * BLOCK
MESH = pl.DeviceIdType.MESH
F32 = jnp.float32
BF16 = jnp.bfloat16
I32 = jnp.int32


def iota(shape, axis):
    return lax.broadcasted_iota(I32, shape, axis)


def column_of(row):
    n = row.shape[1]
    eye = iota((n, n), 0) == iota((n, n), 1)
    return jnp.sum(jnp.where(eye, row, 0), axis=1, keepdims=True)


def row_of(column):
    n = column.shape[0]
    eye = iota((n, n), 0) == iota((n, n), 1)
    return jnp.sum(jnp.where(eye, column, 0), axis=0, keepdims=True)


def kernel(
    n,
    tokens,
    positions,
    lengths,
    gain,
    freq,
    w_query,
    w_key,
    w_value,
    out,
    x,
    normed,
    xs,
    perm,
    wbuf,
    cosine,
    sine,
    send,
    recv,
    code,
    slot,
    slot_row,
    onehot,
    kv,
    bias,
    qs,
    osend,
    tok_sem,
    w_sem,
    send_sem,
    recv_sem,
    halo_send,
    halo_recv,
    out_send,
    out_recv,
):
    groups = n // GROUP
    rows, width = tokens.shape
    per = rows // groups
    total = n * per
    me = lax.axis_index("ctx")
    mine = lax.div(me, GROUP)
    head = lax.rem(me, GROUP)

    tok_chunks = tok_sem.shape[0]
    tok_rows = rows // tok_chunks

    def tok_copy(c):
        part = pl.ds(c * tok_rows, tok_rows)
        return pltpu.make_async_copy(tokens.at[part], x.at[part], tok_sem.at[c])

    for c in range(tok_chunks):
        tok_copy(c).start()

    def head_at(i):
        return lax.rem(head + TURNS[i], GROUP)

    def fetch(k):
        t, i = divmod(k, GROUP)
        if t == 0:
            at = pl.ds(pl.multiple_of(head_at(i) * HEAD, HEAD), HEAD)
            return [
                pltpu.make_async_copy(w.at[:, at], wbuf.at[k, :, pl.ds(c * HEAD, HEAD)], w_sem.at[k])
                for c, w in enumerate((w_key, w_value))
            ]
        at = pl.ds(pl.multiple_of(head_at(i) * 4 * HEAD + (t - 1) * 2 * HEAD, 2 * HEAD), 2 * HEAD)
        return [pltpu.make_async_copy(w_query.at[:, at], wbuf.at[k], w_sem.at[k])]

    def start(k):
        for copy in fetch(k):
            copy.start()

    for k in range(AHEAD):
        start(k)

    barrier = pltpu.get_barrier_semaphore()

    def greet(r, carry):
        pl.semaphore_signal(
            barrier, inc=1, device_id={"ctx": lax.rem(me + r, n)}, device_id_type=MESH
        )
        return carry

    lax.fori_loop(1, n, greet, 0)

    def group_of(where):
        block = lax.shift_right_logical(where, 7)
        return lax.shift_right_logical(jnp.minimum(block, 2 * n - 1 - block), 2)

    here = jnp.concatenate(
        [positions[pl.ds(2 * me, 1), :], positions[pl.ds(2 * me + 1, 1), :]], axis=1
    )
    group_row = group_of(here)
    group_col = column_of(group_row)
    before = (group_col == group_row) & (iota((rows, rows), 0) < iota((rows, rows), 1))
    rank = group_row * per + jnp.sum(before.astype(I32), axis=0, keepdims=True)
    chosen = iota((rows, rows), 0) == rank
    perm[...] = chosen.astype(F32).astype(BF16)
    where_at = jnp.sum(jnp.where(chosen, here, 0), axis=1, keepdims=True)
    angle = where_at.astype(F32) * freq[...]
    sign = jnp.where(iota((1, HEAD), 1) < HEAD // 2, -1.0, 1.0)
    cosine[...] = jnp.cos(angle)
    sine[...] = jnp.sin(angle) * sign

    tiles = width // HEAD
    gains = gain[...].astype(F32)
    for c in range(tok_chunks):
        tok_copy(c).wait()
        part = pl.ds(c * tok_rows, tok_rows)
        square = jnp.zeros((tok_rows, HEAD), F32)
        for j in range(tiles):
            v = x[part, pl.ds(j * HEAD, HEAD)].astype(F32)
            square = square + v * v
        mean = jnp.sum(square, axis=1, keepdims=True) * (1.0 / width)
        scale = lax.rsqrt(mean + EPSILON)
        for j in range(tiles):
            at = pl.ds(j * HEAD, HEAD)
            v = x[part, at].astype(F32) * scale * gains[j : j + 1]
            normed[part, at] = v.astype(BF16)
    step = min(512, width)
    for j in range(width // step):
        at = pl.ds(j * step, step)
        xs[:, at] = jnp.dot(perm[...], normed[:, at], preferred_element_type=F32).astype(BF16)

    def message(t, i, r):
        g = lax.rem(mine + r, groups)
        return send.at[t, i, g], g * GROUP + head_at(i)

    def dispatch(t, i):
        def post(r, carry):
            src, dest = message(t, i, r)
            pltpu.make_async_remote_copy(
                src_ref=src,
                dst_ref=recv.at[t, me],
                send_sem=send_sem.at[t],
                recv_sem=recv_sem.at[t],
                device_id={"ctx": dest},
                device_id_type=MESH,
            ).start()
            return carry

        lax.fori_loop(1, groups, post, 0)
        if i > 0:
            post(0, 0)
        else:
            src, _ = message(t, i, 0)
            pltpu.make_async_copy(src, recv.at[t, me], recv_sem.at[t]).start()

    low_base = mine * RUN
    high_base = (2 * n - GROUP - GROUP * mine) * BLOCK

    def arrange():
        table = positions[...]
        tall = table.shape[0]
        member = group_of(table) == mine
        ones = member.astype(F32)
        upper = (iota((BLOCK, BLOCK), 0) < iota((BLOCK, BLOCK), 1)).astype(F32).astype(BF16)
        ahead = jnp.dot(ones.astype(BF16), upper, preferred_element_type=F32)
        count = jnp.broadcast_to(jnp.sum(ones, axis=1, keepdims=True), ones.shape)
        odd = lax.rem(iota((tall, BLOCK), 0), 2) == 1
        ahead = ahead + jnp.where(odd, pltpu.roll(count, 1, axis=0), 0.0)
        code[...] = jnp.where(member, ahead.astype(I32), -1)
        slot[...] = jnp.where(table < n * BLOCK, table - low_base, table - high_base + RUN)
        together = BLOCK // per
        kth = iota((per, BLOCK), 0)
        for b in range(total // BLOCK):
            parts = []
            for q in range(together):
                found = jnp.zeros((per, BLOCK), I32)
                for e in range(2):
                    line = pl.ds(2 * (b * together + q) + e, 1)
                    found = found + jnp.where(code[line, :] == kth, slot[line, :], 0)
                parts.append(jnp.sum(found, axis=1, keepdims=True))
            column = parts[0] if together == 1 else jnp.concatenate(parts, axis=0)
            slot_row[pl.ds(b, 1), :] = row_of(column)
        lines = iota((BLOCK, BLOCK), 0).astype(F32).astype(BF16)

        def spread(b, carry):
            first = pl.multiple_of(b * BLOCK, BLOCK)
            for j in range(total // BLOCK):
                want = slot_row[pl.ds(j, 1), :] - first
                want = jnp.where((want >= 0) & (want < BLOCK), want, -1)
                want = jnp.broadcast_to(want, (16, BLOCK)).astype(F32).astype(BF16)
                hit = lines == jnp.concatenate([want] * (BLOCK // 16), axis=0)
                onehot[pl.ds(first, BLOCK), pl.ds(j * BLOCK, BLOCK)] = jnp.where(
                    hit, jnp.ones((), BF16), jnp.zeros((), BF16)
                )
            return carry

        lax.fori_loop(0, total // BLOCK, spread, 0)

    for t in range(3):
        for i in range(GROUP):
            k = t * GROUP + i
            pltpu.make_async_copy(wbuf.at[k], wbuf.at[k], w_sem.at[k]).wait()
            if k + AHEAD < 3 * GROUP:
                start(k + AHEAD)
            got = jnp.dot(xs[...], wbuf[k], preferred_element_type=F32)
            for c in range(2):
                u = got[:, c * HEAD : (c + 1) * HEAD]
                if t > 0 or c == 0:
                    u = u * cosine[...] + pltpu.roll(u, HEAD // 2, axis=1) * sine[...]
                send[t, i, :, c] = u.astype(BF16).reshape(groups, per, HEAD)
            if k == GROUP - 1:
                pl.semaphore_wait(barrier, n - 1)
                for j in range(k):
                    dispatch(0, j)
            if k >= GROUP - 1 and k < 3 * GROUP - HELD:
                dispatch(t, i)
            if k == GROUP - 1:
                arrange()

    def arrived(t):
        pltpu.make_async_copy(recv.at[t], recv.at[t], recv_sem.at[t]).wait()
        both = jnp.concatenate(
            [recv[t, :, c].reshape(total, HEAD) for c in range(2)], axis=1
        )
        return both

    both = arrived(0)
    for run in range(2):
        got = jnp.dot(
            onehot[pl.ds(run * RUN, RUN), :], both, preferred_element_type=F32
        ).astype(BF16)
        for c in range(2):
            kv[run, c, pl.ds(REACH, RUN), :] = got[:, c * HEAD : (c + 1) * HEAD]

    tail = pl.ds(RUN, REACH)
    lead = pl.ds(0, REACH)

    def halo(run, dest):
        return pltpu.make_async_remote_copy(
            src_ref=kv.at[run, :, tail],
            dst_ref=kv.at[run, :, lead],
            send_sem=halo_send.at[run],
            recv_sem=halo_recv.at[run],
            device_id={"ctx": dest},
            device_id_type=MESH,
        )

    def halo_start(run, dest):
        for c in range(2):
            for j in range(REACH // HALO_ROWS):
                pltpu.make_async_remote_copy(
                    src_ref=kv.at[run, c, pl.ds(RUN + j * HALO_ROWS, HALO_ROWS)],
                    dst_ref=kv.at[run, c, pl.ds(j * HALO_ROWS, HALO_ROWS)],
                    send_sem=halo_send.at[run],
                    recv_sem=halo_recv.at[run],
                    device_id={"ctx": dest},
                    device_id_type=MESH,
                ).start()

    last = groups - 1

    @pl.when(mine < last)
    def _():
        halo_start(0, me + GROUP)

    @pl.when(mine > 0)
    def _():
        halo_start(1, me - GROUP)

    @pl.when(mine == last)
    def _():
        pltpu.make_async_copy(kv.at[0, :, tail], kv.at[1, :, lead], halo_recv.at[1]).start()

    @pl.when(mine == 0)
    def _():
        for c in range(2):
            kv[0, c, lead, :] = jnp.zeros((REACH, HEAD), BF16)

    for i in range(GROUP - HELD, GROUP):
        dispatch(2, i)

    length_col = column_of(lengths[...])
    docs = lengths.shape[1]
    ends = jnp.sum(
        jnp.where(iota((docs, docs), 0) <= iota((docs, docs), 1), length_col, 0), axis=0, keepdims=True
    )
    for run, base in ((0, low_base), (1, high_base)):

        def fill(b, carry, run=run, base=base):
            at = base + b * BLOCK + iota((BLOCK, 1), 0)
            start = jnp.max(jnp.where(ends <= at, ends, 0), axis=1, keepdims=True)
            key = iota((BLOCK, REACH + BLOCK), 1)
            open_ = (key <= REACH + iota((BLOCK, REACH + BLOCK), 0)) & (
                key >= start - (base + b * BLOCK - REACH)
            )
            bias[run, b] = jnp.where(open_, 0.0, MASKED)
            return carry

        lax.fori_loop(0, GROUP, fill, 0)

    factor = np.float32(np.log2(np.e) / HEAD**0.5)

    def out_copy(t, owner, run):
        src = osend.at[t - 1, owner, run]
        dst = out.at[
            pl.ds(run * BLOCK, BLOCK),
            pl.ds(pl.multiple_of(head * 4 * HEAD + (t - 1) * 2 * HEAD, 2 * HEAD), 2 * HEAD),
        ]
        return src, dst

    for t in (1, 2):
        both = arrived(t)
        for run in range(2):
            got = jnp.dot(
                onehot[pl.ds(run * RUN, RUN), :], both, preferred_element_type=F32
            ).astype(BF16)
            for c in range(2):
                qs[run, c] = got[:, c * HEAD : (c + 1) * HEAD]
        if t == 1:

            @pl.when(mine > 0)
            def _():
                halo(0, me).wait_recv()

            halo(1, me).wait_recv()

        def attend(i, carry, t=t):
            owner = lax.rem(head + 1 + i, GROUP)
            for run in range(2):
                b = owner if run == 0 else GROUP - 1 - owner
                first = pl.multiple_of(b * BLOCK, BLOCK)
                key = kv[run, 0, pl.ds(first, REACH + BLOCK), :]
                value = kv[run, 1, pl.ds(first, REACH + BLOCK), :]
                query = jnp.concatenate([qs[run, c, pl.ds(first, BLOCK), :] for c in range(2)], axis=0)
                s = lax.dot_general(
                    query, key, (((1,), (1,)), ((), ())), preferred_element_type=F32
                )
                mask = bias[run, b]
                s = s + jnp.concatenate([mask, mask], axis=0)
                top = jnp.max(s, axis=1, keepdims=True)
                weights = jnp.exp2((s - top) * factor)
                mass = jnp.sum(weights, axis=1, keepdims=True)
                mixed = jnp.dot(weights.astype(BF16), value, preferred_element_type=F32)
                mixed = (mixed / mass).astype(BF16)
                for c in range(2):
                    osend[t - 1, owner, run, :, pl.ds(c * HEAD, HEAD)] = mixed[
                        c * BLOCK : (c + 1) * BLOCK
                    ]
            for run in range(2):
                src, dst = out_copy(t, owner, run)

                @pl.when(i < GROUP - 1)
                def _(src=src, dst=dst):
                    for j in range(BLOCK // OUT_ROWS):
                        piece = pl.ds(j * OUT_ROWS, OUT_ROWS)
                        pltpu.make_async_remote_copy(
                            src_ref=src.at[piece],
                            dst_ref=dst.at[piece],
                            send_sem=out_send,
                            recv_sem=out_recv,
                            device_id={"ctx": mine * GROUP + owner},
                            device_id_type=MESH,
                        ).start()

                @pl.when(i == GROUP - 1)
                def _(src=src, dst=dst):
                    pltpu.make_async_copy(src, dst, out_recv).start()

            return carry

        lax.fori_loop(0, GROUP, attend, 0)

    pltpu.make_async_copy(out, out, out_recv).wait()
    sent = osend.at[:, pl.ds(0, GROUP - 1)]
    pltpu.make_async_copy(sent, sent, out_send).wait()

    @pl.when(mine < last)
    def _():
        halo(0, me).wait_send()

    @pl.when(mine > 0)
    def _():
        halo(1, me).wait_send()

    for t in range(3):
        done = recv.at[t, pl.ds(0, n - 1)]
        pltpu.make_async_copy(done, done, send_sem.at[t]).wait()


def shards(n, tokens, positions, lengths, gain, w_query, w_key, value_weight):
    rows, width = tokens.shape
    groups = n // GROUP
    per = rows // groups
    total = n * per
    half = HEAD // 2
    freq = (
        np.float32(ROPE_THETA) ** (-(np.arange(half, dtype=np.float32) * 2.0 / HEAD))
    ).astype(np.float32)
    freq = jnp.asarray(np.concatenate([freq, freq])[None])
    vmem = pl.BlockSpec(memory_space=pltpu.VMEM)
    anywhere = pl.BlockSpec(memory_space=pl.ANY)
    sem = pltpu.SemaphoreType.DMA
    return pl.pallas_call(
        functools.partial(kernel, n),
        name="attention",
        out_shape=pltpu.VMEM((rows, w_query.shape[1]), BF16),
        in_specs=[anywhere, vmem, vmem, vmem, vmem, anywhere, anywhere, anywhere],
        out_specs=vmem,
        scratch_shapes=[
            pltpu.VMEM((rows, width), BF16),
            pltpu.VMEM((rows, width), BF16),
            pltpu.VMEM((rows, width), BF16),
            pltpu.VMEM((rows, rows), BF16),
            pltpu.VMEM((3 * GROUP, width, 2 * HEAD), BF16),
            pltpu.VMEM((rows, HEAD), F32),
            pltpu.VMEM((rows, HEAD), F32),
            pltpu.VMEM((3, GROUP, groups, 2, per, HEAD), BF16),
            pltpu.VMEM((3, n, 2, per, HEAD), BF16),
            pltpu.VMEM((2 * n, BLOCK), I32),
            pltpu.VMEM((2 * n, BLOCK), I32),
            pltpu.VMEM((total // BLOCK, BLOCK), I32),
            pltpu.VMEM((total, total), BF16),
            pltpu.VMEM((2, 2, REACH + RUN, HEAD), BF16),
            pltpu.VMEM((2, GROUP, BLOCK, REACH + BLOCK), F32),
            pltpu.VMEM((2, 2, RUN, HEAD), BF16),
            pltpu.VMEM((2, GROUP, 2, BLOCK, 2 * HEAD), BF16),
            sem((4,)),
            sem((3 * GROUP,)),
            sem((3,)),
            sem((3,)),
            sem((2,)),
            sem((2,)),
            sem,
            sem,
        ],
        compiler_params=pltpu.CompilerParams(
            collective_id=0, has_side_effects=True, vmem_limit_bytes=60 * 1024 * 1024
        ),
    )(
        tokens,
        positions.reshape(2 * n, BLOCK),
        lengths.reshape(1, lengths.shape[0]),
        gain.reshape(width // HEAD, HEAD),
        freq,
        w_query,
        w_key,
        value_weight,
    )


def solution(mesh):
    in_specs = (P(("dp", "ctx"), None), P("dp"), P("dp"), P(), P(), P(), P())
    out_specs = P(("dp", "ctx"), None)
    return jax.shard_map(
        functools.partial(shards, mesh.shape["ctx"]),
        mesh=mesh,
        in_specs=in_specs,
        out_specs=out_specs,
        check_vma=False,
    )
```
